256 devices in a mesh: tm: 32 (over y, z), eval: 8 (over x, core).
Axes of the slice: x: 4, y: 4, z: 8, core: 2. Of those that a mesh axis runs over, the one named last changes fastest.
Arguments:
- hidden: bfloat16 [512, 1024, 1536], P('tm', 'eval'), may hold values from -9 to 9
- modulation: float32 [512, 2, 1536], P('tm'), may hold values from -2 to 3
- head_weight: bfloat16 [64, 1536], replicated, may hold values from -1 to 1
- real_score: bfloat16 [64, 21, 16, 4096], P('eval', None, None, 'tm'), may hold values from -152917 to 152917
- fake_score: bfloat16 [64, 21, 16, 4096], P('eval', None, None, 'tm'), may hold values from -152917 to 152917
- window_start: int32 [64], P('eval'), may hold values from 0 to 491, as said below
- timestep: int32 [64], P('eval'), may hold values from 20 to 999
Outputs:
- d_hidden: bfloat16 [512, 1024, 1536], P('tm', 'eval')
- head_grad: float32 [64, 1536], replicated
- mod_grad: float32 [512, 2, 1536], P('tm')
The draws below stay inside these ranges and needn't reach their ends.
Inputs may be any that keep to these rules, and one draw needn't show every extreme that they name: `window_start`: every window lies inside the rollout; one window starts at frame 0 and one at the last possible frame.
All inputs are finite; a program needn't handle non-finite values.
Results may differ from the reference program's by a relative error of at most 0.0012.
The reference program's roundings to bfloat16 on the way (of `adapted`, `latent` and `upstream`) count: a program that leaves them out, or rounds other values in their place, can miss the bound.
Values may be sent and summed in bfloat16 or wider, within the bound.
No kernel may reach another device: no remote copies, remote signals or barrier semaphores. Data moves between devices by JAX's collectives and lax.ppermute only.
A program may use at most 128 MiB of HBM per device.

```python
import math
import jax
import jax.numpy as jnp
from jax import lax

D = 1536
C = 16
PATCH = 4
WIN = 21
FD = 16
TOK = 1024
NW_DEV = 8
NWIN = 64
N_TM = 32
N_EVAL = 8


spike_count = 24


def spike_field(key):
    count = NW_DEV * N_EVAL
    entries = WIN * C * TOK * PATCH
    stratum = entries // spike_count
    offsets = jax.random.randint(jax.random.fold_in(key, 41), (count, spike_count), 0, stratum)
    spots = (jnp.arange(spike_count, dtype=jnp.int32)[None, :] * stratum + offsets).astype(jnp.int32)
    signs = (jax.random.randint(jax.random.fold_in(key, 42), (count, spike_count), 0, 2) * 2 - 1).astype(jnp.float32)
    levels = jnp.exp(jax.random.uniform(jax.random.fold_in(key, 43), (count, spike_count), jnp.float32, 0.0, math.log(10.0))) * (math.log(10.0) / 9.0)
    amounts = signs * levels * (0.04 * entries)
    return (spots, amounts)


def place_spikes(key, base):
    count = NW_DEV * N_EVAL
    spots, amounts = spike_field(key)
    window_rows = jnp.arange(count, dtype=jnp.int32)[:, None]
    flat = base.reshape(count, WIN * C * TOK * PATCH).at[window_rows, spots].set(amounts)
    return flat.reshape(base.shape).astype(jnp.bfloat16)


def shared_direction(key):
    bits = jax.random.randint(jax.random.fold_in(key, 51), (D,), 0, 2)
    return (bits * 2 - 1).astype(jnp.float32)


def draw_hidden(key, part):
    shape = (FD * N_TM, TOK, D)
    direction = shared_direction(key)
    noise = jnp.clip(jax.random.normal(jax.random.fold_in(key, 53), shape, jnp.float32), -6.0, 6.0)
    strength = 3.0 * jnp.arange(TOK, dtype=jnp.float32) / TOK
    values = noise + strength[None, :, None] * direction[None, None, :]
    return values.astype(jnp.bfloat16)


def draw_head_weight(key, part):
    direction = shared_direction(key)
    base = jnp.clip(jax.random.normal(jax.random.fold_in(key, 54), (C * PATCH, D), jnp.float32), -6.0, 6.0)
    loads = jnp.clip(jax.random.normal(jax.random.fold_in(key, 55), (C * PATCH,), jnp.float32), -3.0, 3.0)
    values = base / math.sqrt(D) + 2.0 * loads[:, None] * direction[None, :] / D
    return values.astype(jnp.bfloat16)


def draw_modulation(key, part):
    frames = FD * N_TM
    levels = jnp.exp(jax.random.uniform(jax.random.fold_in(key, 61), (frames, 1), jnp.float32, math.log(0.3), math.log(3.0)))
    scale_noise = 0.3 * jnp.clip(jax.random.normal(jax.random.fold_in(key, 64), (frames, D), jnp.float32), -3.0, 3.0)
    shift = 0.5 * jnp.clip(jax.random.normal(jax.random.fold_in(key, 65), (frames, D), jnp.float32), -3.0, 3.0)
    scale = levels - 1.0 + scale_noise
    return jnp.stack([shift, scale], axis=1).astype(jnp.float32)


def draw_real_score(key, part):
    shape = (NW_DEV * N_EVAL, WIN, C, TOK * PATCH)
    ramp = 1.0 + 2.0 * jnp.arange(TOK * PATCH, dtype=jnp.float32) / (TOK * PATCH)
    values = jnp.clip(jax.random.normal(jax.random.fold_in(key, 13), shape, jnp.float32), -6.0, 6.0)
    base = values * ramp
    return place_spikes(key, base)


def draw_fake_score(key, part):
    shape = (NW_DEV * N_EVAL, WIN, C, TOK * PATCH)
    base = jnp.clip(jax.random.normal(jax.random.fold_in(key, 15), shape, jnp.float32), -6.0, 6.0)
    return place_spikes(key, base)


def draw_window_start(key, part):
    count = NW_DEV * N_EVAL
    limit = FD * N_TM - WIN
    starts = jax.random.randint(jax.random.fold_in(key, 21), (count,), 0, limit + 1)
    starts = starts.at[0].set(0)
    starts = starts.at[count - 1].set(limit)
    return starts.astype(jnp.int32)


def with_ends(result, own_key, smallest, high):
    longest = result.shape.index(max(result.shape))
    spots = []
    for shift in (0, 1):
        where = [jax.random.randint(jax.random.fold_in(own_key, axis), (), 0, length) for axis, length in enumerate(result.shape)]
        where[longest] = (where[longest] + shift) % result.shape[longest]
        spots.append(tuple(where))
    return result.at[spots[0]].set(smallest).at[spots[1]].set(high)


def setup_inputs(seed: int = 0) -> dict:
    splits = jax.random.split(jax.random.key(seed), 8)
    hidden = draw_hidden(jax.random.fold_in(splits[7], 71), 0)
    modulation = draw_modulation(jax.random.fold_in(splits[7], 71), 0)
    head_weight = draw_head_weight(jax.random.fold_in(splits[7], 71), 0)
    real_score = draw_real_score(jax.random.fold_in(splits[7], 71), 0)
    fake_score = draw_fake_score(jax.random.fold_in(splits[7], 71), 0)
    window_start = draw_window_start(jax.random.fold_in(splits[7], 71), 0)
    timestep = with_ends(jax.random.randint(splits[6], (NWIN,), 20, 1000), jax.random.fold_in(splits[6], 1), 20, 999).astype(jnp.int32)
    return dict(hidden=hidden, modulation=modulation, head_weight=head_weight, real_score=real_score, fake_score=fake_score, window_start=window_start, timestep=timestep)


def layer_norm(frame):
    values = frame.astype(jnp.float32)
    center = lax.optimization_barrier(jnp.mean(values, axis=-1, keepdims=True))
    shifted = values - center
    inv_std = lax.rsqrt(lax.optimization_barrier(jnp.mean(shifted * shifted, axis=-1, keepdims=True)) + 1e-06)
    return (shifted * inv_std, inv_std)

def reference(hidden, modulation, head_weight, real_score, fake_score, window_start, timestep):

    def forward(pair):
        frame, shift_scale = pair
        normed, inv_std = layer_norm(frame)
        adapted = (normed * (1.0 + shift_scale[1]) + shift_scale[0]).astype(jnp.bfloat16)
        output = jnp.dot(adapted, head_weight.T, preferred_element_type=jnp.float32)
        return output.astype(jnp.bfloat16).reshape(TOK, C, PATCH).transpose(1, 0, 2).reshape(C, TOK * PATCH)
    latent = lax.map(forward, (hidden, modulation))

    def add_window(total, items):
        start, level, real, fake = items
        start = start.astype(jnp.int32)
        block = lax.dynamic_slice_in_dim(latent, start, WIN, 0).astype(jnp.float32)
        real_values = real.astype(jnp.float32)
        fake_values = fake.astype(jnp.float32)
        normalizer = jnp.sum(jnp.abs(block - real_values)) / (WIN * C * PATCH * TOK) + 1e-05
        weight = level.astype(jnp.float32) / 1000.0 / normalizer
        window_grad = weight * (fake_values - real_values)
        current = lax.dynamic_slice_in_dim(total, start, WIN, 0)
        return (lax.dynamic_update_slice_in_dim(total, current + window_grad, start, 0), None)
    empty = jnp.zeros((FD * N_TM, C, TOK * PATCH), jnp.float32)
    frame_grad, _ = lax.scan(add_window, empty, (window_start, timestep, real_score, fake_score))

    def backward(total, items):
        frame, shift_scale, grad = items
        normed, inv_std = layer_norm(frame)
        adapted = (normed * (1.0 + shift_scale[1]) + shift_scale[0]).astype(jnp.bfloat16)
        upstream = grad.reshape(C, TOK, PATCH).transpose(1, 0, 2).reshape(TOK, C * PATCH).astype(jnp.bfloat16)
        d_adapted = jnp.dot(upstream, head_weight, preferred_element_type=jnp.float32)
        head_part = jnp.dot(upstream.T, adapted, preferred_element_type=jnp.float32)
        mod_part = jnp.stack([lax.optimization_barrier(jnp.sum(d_adapted, axis=0)), lax.optimization_barrier(jnp.sum(d_adapted * normed, axis=0))])
        d_normed = d_adapted * (1.0 + shift_scale[1])
        d_hidden = inv_std * (d_normed - lax.optimization_barrier(jnp.mean(d_normed, axis=-1, keepdims=True)) - normed * lax.optimization_barrier(jnp.mean(d_normed * normed, axis=-1, keepdims=True)))
        return (total + head_part, (d_hidden.astype(jnp.bfloat16), mod_part))
    start_head = jnp.zeros((C * PATCH, hidden.shape[2]), jnp.float32)
    head_grad, (d_hidden, mod_grad) = lax.scan(backward, start_head, (hidden, modulation, frame_grad))
    return (d_hidden, head_grad, mod_grad)
```

```python
import functools
import jax
import jax.numpy as jnp
from jax import lax
from jax.experimental import pallas as pl
from jax.experimental.pallas import tpu as pltpu
from jax.sharding import PartitionSpec as P

C = 16
PATCH = 4
OUT = C * PATCH
WIN = 21
TOK = 1024
D = 1536
NTM = 32
NEV = 8
FD = 16
TD = TOK // NEV
PX = TD * PATCH
NF = FD * NTM
BLK = PX // PATCH
G = 2
NW = 8
HEAD_ROWS = OUT // NEV
MOD_ROWS = 2 * FD // NEV
ROWS = HEAD_ROWS + MOD_ROWS


F32 = jnp.float32
BF16 = jnp.bfloat16


def params(**more):
    return pltpu.CompilerParams(vmem_limit_bytes=56 * 1024 * 1024, **more)


def dot(a, b, ca=1, cb=0):
    return lax.dot_general(a, b, (((ca,), (cb,)), ((), ())), preferred_element_type=F32)


def build_weight(w_ref, wp_ref):
    row = lax.broadcasted_iota(jnp.int32, (OUT, OUT), 0)
    col = lax.broadcasted_iota(jnp.int32, (OUT, OUT), 1)
    pick = (col == (row % C) * PATCH + row // C).astype(F32).astype(BF16)
    wp_ref[...] = dot(pick, w_ref[...]).astype(BF16)


def build_pixels(e_ref, turn):
    row = lax.broadcasted_iota(jnp.int32, (PX, PX), 0)
    col = lax.broadcasted_iota(jnp.int32, (PX, PX), 1)
    pixel = (col + turn * BLK) % PX
    e_ref[...] = (pixel == (row % TD) * PATCH + row // TD).astype(F32).astype(BF16)


def forward_kernel(x_ref, mod_ref, w_ref, ad_ref, st_ref, l0_ref, l1_ref, l2_ref, l3_ref, wp_ref, e_ref):
    @pl.when(pl.program_id(0) == 0)
    def _():
        build_weight(w_ref, wp_ref)
        build_pixels(e_ref, lax.axis_index("tm") % 4)

    lane = lax.broadcasted_iota(jnp.int32, (TD, 128), 1)
    for g in range(G):
        x = x_ref[g].astype(F32)
        m = jnp.mean(x, axis=-1, keepdims=True)
        xc = x - m
        inv = lax.rsqrt(jnp.mean(xc * xc, axis=-1, keepdims=True) + 1e-06)
        st_ref[g] = jnp.where(lane == 0, m, inv)
        ad = ((xc * inv) * (1.0 + mod_ref[g, 1:2, :]) + mod_ref[g, 0:1, :]).astype(BF16)
        ad_ref[g] = ad
        o = dot(wp_ref[...], ad, 1, 1).astype(BF16)
        wide = jnp.concatenate([o[s * C : (s + 1) * C] for s in range(PATCH)], axis=1)
        lat = dot(wide, e_ref[...]).astype(BF16)
        for r, ref in enumerate((l0_ref, l1_ref, l2_ref, l3_ref)):
            ref[g] = lat[:, r * BLK : (r + 1) * BLK]


def forward(hidden, modulation, weight):
    piece = jax.ShapeDtypeStruct((FD, C, BLK), BF16)
    return pl.pallas_call(
        forward_kernel,
        grid=(FD // G,),
        in_specs=[
            pl.BlockSpec((G, TD, D), lambda i: (i, 0, 0)),
            pl.BlockSpec((G, 2, D), lambda i: (i, 0, 0)),
            pl.BlockSpec((OUT, D), lambda i: (0, 0)),
        ],
        out_specs=[
            pl.BlockSpec((G, TD, D), lambda i: (i, 0, 0)),
            pl.BlockSpec((G, TD, 128), lambda i: (i, 0, 0)),
        ]
        + [pl.BlockSpec((G, C, BLK), lambda i: (i, 0, 0))] * 4,
        out_shape=[
            jax.ShapeDtypeStruct((FD, TD, D), BF16),
            jax.ShapeDtypeStruct((FD, TD, 128), F32),
        ]
        + [piece] * 4,
        scratch_shapes=[pltpu.VMEM((OUT, D), BF16), pltpu.VMEM((PX, PX), BF16)],
        compiler_params=params(),
        name="forward",
    )(hidden, modulation, weight)


def row_of(frame, tm):
    y, zj = tm // 8, tm % 4
    owner = frame // FD
    yo, co, jo = owner // 8, (owner // 4) % 2, owner % 4
    block = 2 * ((yo + y) % 4) + co
    return 64 * block + FD * ((zj + 4 - jo) % 4) + frame % FD


def sums_kernel(start_ref, lat_ref, real_ref, out_ref):
    tm = lax.axis_index("tm")
    lane = lax.broadcasted_iota(jnp.int32, (1, 128), 1)
    total = jnp.zeros((1, 128), F32)
    for w in range(NW):
        start = start_ref[w]
        acc = jnp.zeros((C, 128), F32)
        for t in range(WIN):
            row = row_of(start + t, tm)
            acc += jnp.abs(lat_ref[row].astype(F32) - real_ref[w, t].astype(F32))
        total = jnp.where(lane == w, jnp.sum(acc), total)
    out_ref[...] = jnp.broadcast_to(total[None], (NTM, 1, 128))


def window_sums(starts, latents, real):
    return pl.pallas_call(
        sums_kernel,
        in_specs=[
            pl.BlockSpec(memory_space=pltpu.SMEM),
            pl.BlockSpec(memory_space=pltpu.VMEM),
            pl.BlockSpec(memory_space=pltpu.VMEM),
        ],
        out_specs=pl.BlockSpec(memory_space=pltpu.VMEM),
        out_shape=jax.ShapeDtypeStruct((NTM, 1, 128), F32),
        compiler_params=params(),
        name="window_sums",
    )(starts, latents, real)


def grads_kernel(start_ref, step_ref, tot_ref, real_ref, fake_ref, out_ref):
    tm = lax.axis_index("tm")
    lane = lax.broadcasted_iota(jnp.int32, (1, 128), 1)
    totals = jnp.sum(tot_ref[...], axis=0)
    normalizer = totals / (WIN * C * PATCH * TOK) + 1e-05
    level = jnp.zeros((1, 128), F32)
    for w in range(NW):
        level = jnp.where(lane == w, step_ref[w].astype(F32), level)
    weight = level / 1000.0 / normalizer
    out_ref[...] = jnp.zeros_like(out_ref)
    for w in range(NW):
        start = start_ref[w]
        one = jnp.sum(jnp.where(lane == w, weight, 0.0), axis=1, keepdims=True)
        for t in range(WIN):
            row = row_of(start + t, tm)
            out_ref[row] += one * (fake_ref[w, t].astype(F32) - real_ref[w, t].astype(F32))


def window_grads(starts, steps, totals, real, fake):
    smem = pl.BlockSpec(memory_space=pltpu.SMEM)
    vmem = pl.BlockSpec(memory_space=pltpu.VMEM)
    return pl.pallas_call(
        grads_kernel,
        in_specs=[smem, smem, vmem, vmem, vmem],
        out_specs=vmem,
        out_shape=jax.ShapeDtypeStruct((NF, C, BLK), F32),
        compiler_params=params(),
        name="window_grads",
    )(starts, steps, totals, real, fake)


def backward_kernel(
    x_ref, st_ref, ad_ref, mod_ref, w_ref, g0_ref, g1_ref, g2_ref, g3_ref, dh_ref, red_ref, wp_ref, e_ref, acc_ref
):
    step = pl.program_id(0)

    @pl.when(step == 0)
    def _():
        build_weight(w_ref, wp_ref)
        build_pixels(e_ref, lax.axis_index("tm") % 4)
        acc_ref[...] = jnp.zeros_like(acc_ref)

    ups = []
    for g in range(G):
        grad = jnp.concatenate([ref[g] for ref in (g0_ref, g1_ref, g2_ref, g3_ref)], axis=1)
        wide = dot(grad, e_ref[...], 1, 1).astype(BF16)
        ups.append(jnp.concatenate([wide[:, s * TD : (s + 1) * TD] for s in range(PATCH)], axis=0))
    both = jnp.concatenate(ups, axis=1)
    acc_ref[...] += dot(both, ad_ref[...].reshape(G * TD, D))
    for g in range(G):
        d_ad = dot(ups[g], wp_ref[...], 0, 0)
        m = st_ref[g, :, 0:1]
        inv = st_ref[g, :, 1:2]
        normed = (x_ref[g].astype(F32) - m) * inv
        red_ref[step, HEAD_ROWS + 2 * g : HEAD_ROWS + 2 * g + 1, :] = jnp.sum(d_ad, axis=0, keepdims=True)
        red_ref[step, HEAD_ROWS + 2 * g + 1 : HEAD_ROWS + 2 * g + 2, :] = jnp.sum(
            d_ad * normed, axis=0, keepdims=True
        )
        dn = d_ad * (1.0 + mod_ref[g, 1:2, :])
        m1 = jnp.mean(dn, axis=-1, keepdims=True)
        m2 = jnp.mean(dn * normed, axis=-1, keepdims=True)
        dh_ref[g] = (inv * (dn - m1 - normed * m2)).astype(BF16)

    @pl.when(step == pl.num_programs(0) - 1)
    def _():
        for c in range(C):
            for s in range(PATCH):
                row = PATCH * c + s
                red_ref[row // HEAD_ROWS, row % HEAD_ROWS : row % HEAD_ROWS + 1, :] = acc_ref[
                    s * C + c : s * C + c + 1, :
                ]


def backward(hidden, stats, adapted, modulation, weight, pieces):
    return pl.pallas_call(
        backward_kernel,
        grid=(FD // G,),
        in_specs=[
            pl.BlockSpec((G, TD, D), lambda i: (i, 0, 0)),
            pl.BlockSpec((G, TD, 128), lambda i: (i, 0, 0)),
            pl.BlockSpec((G, TD, D), lambda i: (i, 0, 0)),
            pl.BlockSpec((G, 2, D), lambda i: (i, 0, 0)),
            pl.BlockSpec((OUT, D), lambda i: (0, 0)),
        ]
        + [pl.BlockSpec((G, C, BLK), lambda i: (i, 0, 0))] * 4,
        out_specs=[
            pl.BlockSpec((G, TD, D), lambda i: (i, 0, 0)),
            pl.BlockSpec((NEV, ROWS, D), lambda i: (0, 0, 0)),
        ],
        out_shape=[
            jax.ShapeDtypeStruct((FD, TD, D), BF16),
            jax.ShapeDtypeStruct((NEV, ROWS, D), F32),
        ],
        scratch_shapes=[
            pltpu.VMEM((OUT, D), BF16),
            pltpu.VMEM((PX, PX), BF16),
            pltpu.VMEM((OUT, D), F32),
        ],
        compiler_params=params(),
        name="backward",
    )(hidden, stats, adapted, modulation, weight, *pieces)


def skew(r):
    pairs = []
    for tm in range(NTM):
        for ev in range(NEV):
            y, z = divmod(tm, 8)
            x, c = divmod(ev, 2)
            dest_tm = 8 * x + 4 * c + (z + r) % 4
            dest_ev = 2 * ((x + y) % 4) + z // 4
            pairs.append((tm * NEV + ev, dest_tm * NEV + dest_ev))
    return pairs


def per_device(hidden, modulation, head_weight, real_score, fake_score, window_start, timestep):
    both = ("tm", "eval")
    adapted, stats, *pieces = forward(hidden, modulation, head_weight)
    moved = [lax.ppermute(piece, both, skew(r)) for r, piece in enumerate(pieces)]
    held = jnp.concatenate(moved, axis=0)
    latents = lax.all_gather(held, "eval", axis=0, tiled=True)
    sums = window_sums(window_start, latents, real_score)
    totals = lax.all_to_all(sums, "tm", split_axis=0, concat_axis=0, tiled=True)
    group = window_grads(window_start, timestep, totals, real_score, fake_score)
    mine = lax.psum_scatter(group, "eval", scatter_dimension=0, tiled=True).astype(BF16)
    back = []
    for r in range(4):
        inverse = [(b, a) for a, b in skew(r)]
        back.append(lax.ppermute(mine[FD * r : FD * (r + 1)], both, inverse))
    d_hidden, parts = backward(hidden, stats, adapted, modulation, head_weight, back)
    mixed = lax.all_to_all(parts, "eval", split_axis=0, concat_axis=0, tiled=True)
    own = jnp.sum(mixed, axis=0)
    head = own[:HEAD_ROWS]
    for bit in (1, 2, 4, 8, 16):
        head = head + lax.ppermute(head, "tm", [(i, i ^ bit) for i in range(NTM)])
    own = jnp.concatenate([head, own[HEAD_ROWS:]], axis=0)
    spread = jnp.broadcast_to(own[None], (NEV, ROWS, D))
    whole = lax.all_to_all(spread, "eval", split_axis=0, concat_axis=0, tiled=True)
    head_grad = whole[:, :HEAD_ROWS].reshape(OUT, D)
    mod_grad = whole[:, HEAD_ROWS:].reshape(FD, 2, D)
    return (d_hidden, head_grad, mod_grad)


def solution(mesh):
    placed = (
        P("tm", "eval", None),
        P("tm", None, None),
        P(),
        P("eval", None, None, "tm"),
        P("eval", None, None, "tm"),
        P("eval"),
        P("eval"),
    )
    return jax.shard_map(
        per_device,
        mesh=mesh,
        in_specs=placed,
        out_specs=(P("tm", "eval", None), P(), P("tm", None, None)),
        check_vma=False,
    )
```

```python
import jax
import jax.numpy as jnp
from jax import lax
from jax.experimental import pallas as pl
from jax.experimental.pallas import tpu as pltpu
from jax.sharding import PartitionSpec as P

C = 16
PATCH = 4
OUT = C * PATCH
WIN = 21
TOK = 1024
D = 1536
NTM = 32
NEV = 8
FD = 16
TD = TOK // NEV
PX = TD * PATCH
NF = FD * NTM
BLK = PX // PATCH
G = 2
ROW = 16
PARTS = 4
NW = 8
HEAD_ROWS = OUT // NEV


F32 = jnp.float32
BF16 = jnp.bfloat16


def params(**more):
    return pltpu.CompilerParams(vmem_limit_bytes=56 * 1024 * 1024, **more)


def dot(a, b, ca=1, cb=0):
    return lax.dot_general(a, b, (((ca,), (cb,)), ((), ())), preferred_element_type=F32)


def build_weight(w_ref, wp_ref):
    row = lax.broadcasted_iota(jnp.int32, (OUT, OUT), 0)
    col = lax.broadcasted_iota(jnp.int32, (OUT, OUT), 1)
    pick = (col == (row % C) * PATCH + row // C).astype(F32).astype(BF16)
    wp_ref[...] = dot(pick, w_ref[...]).astype(BF16)


def build_pixels(e_ref):
    row = lax.broadcasted_iota(jnp.int32, (PX, PX), 0)
    col = lax.broadcasted_iota(jnp.int32, (PX, PX), 1)
    e_ref[...] = (col == (row % TD) * PATCH + row // TD).astype(F32).astype(BF16)


def forward_kernel(x_ref, mod_ref, w_ref, ad_ref, st_ref, lat_ref, wp_ref, e_ref):
    @pl.when(pl.program_id(0) == 0)
    def _():
        build_weight(w_ref, wp_ref)
        build_pixels(e_ref)

    lane = lax.broadcasted_iota(jnp.int32, (ROW, 128), 1)
    for g in range(G):
        scale = 1.0 + mod_ref[g, 1:2, :]
        shift = mod_ref[g, 0:1, :]
        for q in range(0, TD, ROW):
            x = x_ref[g, q : q + ROW, :].astype(F32)
            m = jnp.mean(x, axis=-1, keepdims=True)
            xc = x - m
            inv = lax.rsqrt(jnp.mean(xc * xc, axis=-1, keepdims=True) + 1e-06)
            st_ref[g, q : q + ROW, :] = jnp.where(lane == 0, m, inv)
            ad_ref[g, q : q + ROW, :] = ((xc * inv) * scale + shift).astype(BF16)
        o = dot(wp_ref[...], ad_ref[g], 1, 1).astype(BF16)
        wide = jnp.concatenate([o[s * C : (s + 1) * C] for s in range(PATCH)], axis=1)
        lat = dot(wide, e_ref[...]).astype(BF16)
        for k in range(4):
            lat_ref[k, g] = lat[:, k * BLK : (k + 1) * BLK]


def forward(hidden, modulation, weight):
    return pl.pallas_call(
        forward_kernel,
        grid=(FD // G,),
        in_specs=[
            pl.BlockSpec((G, TD, D), lambda i: (i, 0, 0)),
            pl.BlockSpec((G, 2, D), lambda i: (i, 0, 0)),
            pl.BlockSpec((OUT, D), lambda i: (0, 0)),
        ],
        out_specs=[
            pl.BlockSpec((G, TD, D), lambda i: (i, 0, 0)),
            pl.BlockSpec((G, TD, 128), lambda i: (i, 0, 0)),
            pl.BlockSpec((4, G, C, BLK), lambda i: (0, i, 0, 0)),
        ],
        out_shape=[
            jax.ShapeDtypeStruct((FD, TD, D), BF16),
            jax.ShapeDtypeStruct((FD, TD, 128), F32),
            jax.ShapeDtypeStruct((4, FD, C, BLK), BF16),
        ],
        scratch_shapes=[pltpu.VMEM((OUT, D), BF16), pltpu.VMEM((PX, PX), BF16)],
        compiler_params=params(),
        name="forward",
    )(hidden, modulation, weight)


def row_table(starts):
    y = lax.axis_index("tm") // 8
    core = lax.axis_index("eval") % 2
    frame = starts[:, None] + jnp.arange(WIN, dtype=jnp.int32)[None, :]
    block = frame // 64
    half = (block % 2 + core) % 2
    return half * (NF // 2) + 64 * ((block // 2 + y) % 4) + frame % 64


def sums_kernel(row_ref, own_ref, other_ref, real_ref, out_ref, lat_ref, sem):
    copies = [
        pltpu.make_async_copy(own_ref, lat_ref.at[pl.ds(0, NF // 2)], sem.at[0]),
        pltpu.make_async_copy(other_ref, lat_ref.at[pl.ds(NF // 2, NF // 2)], sem.at[1]),
    ]
    for copy in copies:
        copy.start()
    for copy in copies:
        copy.wait()
    rows = []
    for w in range(NW):
        parts = [
            jnp.abs(lat_ref[row_ref[w, t]].astype(F32) - real_ref[w, t].astype(F32)) for t in range(WIN)
        ]
        while len(parts) > 1:
            parts = [a + b for a, b in zip(parts[::2], parts[1::2])] + ([parts[-1]] if len(parts) % 2 else [])
        rows.append(jnp.sum(parts[0], axis=0, keepdims=True))
    each = jnp.sum(jnp.concatenate(rows, axis=0), axis=1, keepdims=True)
    lane = lax.broadcasted_iota(jnp.int32, (NW, 128), 1)
    place = lax.broadcasted_iota(jnp.int32, (NW, 128), 0)
    total = jnp.sum(jnp.where(lane == place, each, 0.0), axis=0, keepdims=True)
    out_ref[...] = jnp.broadcast_to(total[None], (NTM, 1, 128))


def window_sums(rows, own, other, real):
    return pl.pallas_call(
        sums_kernel,
        in_specs=[
            pl.BlockSpec(memory_space=pltpu.SMEM),
            pl.BlockSpec(memory_space=pl.ANY),
            pl.BlockSpec(memory_space=pl.ANY),
            pl.BlockSpec(memory_space=pltpu.VMEM),
        ],
        out_specs=pl.BlockSpec(memory_space=pltpu.VMEM),
        out_shape=jax.ShapeDtypeStruct((NTM, 1, 128), F32),
        scratch_shapes=[pltpu.VMEM((NF, C, BLK), BF16), pltpu.SemaphoreType.DMA((2,))],
        compiler_params=params(),
        name="window_sums",
    )(rows, own, other, real)


def grads_kernel(row_ref, step_ref, tot_ref, real_ref, fake_ref, own_ref, other_ref, acc_ref, sem):
    lane = lax.broadcasted_iota(jnp.int32, (1, 128), 1)
    totals = jnp.sum(tot_ref[...], axis=0)
    normalizer = totals / (WIN * C * PATCH * TOK) + 1e-05
    level = jnp.zeros((1, 128), F32)
    for w in range(NW):
        level = jnp.where(lane == w, step_ref[w].astype(F32), level)
    weight = level / 1000.0 / normalizer
    acc_ref[...] = jnp.zeros_like(acc_ref)
    for w in range(NW):
        one = jnp.sum(jnp.where(lane == w, weight, 0.0), axis=1, keepdims=True)
        for t in range(WIN):
            acc_ref[row_ref[w, t]] += one * (fake_ref[w, t].astype(F32) - real_ref[w, t].astype(F32))
    copies = [
        pltpu.make_async_copy(acc_ref.at[pl.ds(NF // 2, NF // 2)], other_ref, sem.at[1]),
        pltpu.make_async_copy(acc_ref.at[pl.ds(0, NF // 2)], own_ref, sem.at[0]),
    ]
    for copy in copies:
        copy.start()
    for copy in copies:
        copy.wait()


def window_grads(rows, steps, totals, real, fake):
    smem = pl.BlockSpec(memory_space=pltpu.SMEM)
    vmem = pl.BlockSpec(memory_space=pltpu.VMEM)
    half = jax.ShapeDtypeStruct((NF // 2, C, BLK), F32)
    return pl.pallas_call(
        grads_kernel,
        in_specs=[smem, smem, vmem, vmem, vmem],
        out_specs=[pl.BlockSpec(memory_space=pl.ANY)] * 2,
        out_shape=[half, half],
        scratch_shapes=[pltpu.VMEM((NF, C, BLK), F32), pltpu.SemaphoreType.DMA((2,))],
        compiler_params=params(),
        name="window_grads",
    )(rows, steps, totals, real, fake)


def place_of(device):
    rel = lax.bitwise_xor(lax.axis_index("eval"), device)
    return 4 * (rel % 2) + 2 * ((rel // 2) % 2) + rel // 4


def head_kernel(g_ref, ad_ref, up_ref, head_ref, e_ref, acc_ref):
    step = pl.program_id(0)

    @pl.when(step == 0)
    def _():
        build_pixels(e_ref)
        acc_ref[...] = jnp.zeros_like(acc_ref)

    ups = []
    for g in range(G):
        grad = jnp.concatenate([g_ref[k, g] for k in range(4)], axis=1)
        wide = dot(grad, e_ref[...], 1, 1).astype(BF16)
        up = jnp.concatenate([wide[:, s * TD : (s + 1) * TD] for s in range(PATCH)], axis=0)
        up_ref[g] = up
        ups.append(up)
    acc_ref[...] += dot(jnp.concatenate(ups, axis=1), ad_ref[...].reshape(G * TD, D))

    @pl.when(step == pl.num_programs(0) - 1)
    def _():
        for e in range(NEV):
            place = place_of(e)
            for i in range(HEAD_ROWS):
                c, s = divmod(e * HEAD_ROWS + i, PATCH)
                head_ref[place, i : i + 1, :] = acc_ref[s * C + c : s * C + c + 1, :]


def head_part(pieces, adapted):
    return pl.pallas_call(
        head_kernel,
        grid=(FD // G,),
        in_specs=[
            pl.BlockSpec((4, G, C, BLK), lambda i: (0, i, 0, 0)),
            pl.BlockSpec((G, TD, D), lambda i: (i, 0, 0)),
        ],
        out_specs=[
            pl.BlockSpec((G, OUT, TD), lambda i: (i, 0, 0)),
            pl.BlockSpec((NEV, HEAD_ROWS, D), lambda i: (0, 0, 0)),
        ],
        out_shape=[
            jax.ShapeDtypeStruct((FD, OUT, TD), BF16),
            jax.ShapeDtypeStruct((NEV, HEAD_ROWS, D), F32),
        ],
        scratch_shapes=[pltpu.VMEM((PX, PX), BF16), pltpu.VMEM((OUT, D), F32)],
        compiler_params=params(),
        name="head_part",
    )(pieces, adapted)


def hidden_kernel(x_ref, st_ref, up_ref, mod_ref, w_ref, *refs):
    dh_ref, red_ref, wp_ref, da_ref = refs[-4:]

    @pl.when(pl.program_id(0) == 0)
    def _():
        build_weight(w_ref, wp_ref)

    for g in range(G):
        da_ref[...] = dot(up_ref[g], wp_ref[...], 0, 0)
        scale = 1.0 + mod_ref[g, 1:2, :]
        sum0 = jnp.zeros((ROW, D), F32)
        sum1 = jnp.zeros((ROW, D), F32)
        for q in range(0, TD, ROW):
            d_ad = da_ref[q : q + ROW, :]
            inv = st_ref[g, q : q + ROW, 1:2]
            normed = (x_ref[g, q : q + ROW, :].astype(F32) - st_ref[g, q : q + ROW, 0:1]) * inv
            product = d_ad * normed
            sum0 += d_ad
            sum1 += product
            dn = d_ad * scale
            m1 = jnp.mean(dn, axis=-1, keepdims=True)
            m2 = jnp.mean(product * scale, axis=-1, keepdims=True)
            dh_ref[g, q : q + ROW, :] = (inv * (dn - m1 - normed * m2)).astype(BF16)
        red_ref[g, 0:1, :] = jnp.sum(sum0, axis=0, keepdims=True)
        red_ref[g, 1:2, :] = jnp.sum(sum1, axis=0, keepdims=True)


def hidden_part(part, hidden, stats, up, modulation, weight, so_far):
    count = FD // PARTS // G
    at = part * count
    shapes = [jax.ShapeDtypeStruct((FD, TD, D), BF16), jax.ShapeDtypeStruct((FD // PARTS, 2, D), F32)]
    more = [] if so_far is None else [so_far]
    return pl.pallas_call(
        hidden_kernel,
        grid=(count,),
        in_specs=[
            pl.BlockSpec((G, TD, D), lambda i: (i + at, 0, 0)),
            pl.BlockSpec((G, TD, 128), lambda i: (i + at, 0, 0)),
            pl.BlockSpec((G, OUT, TD), lambda i: (i + at, 0, 0)),
            pl.BlockSpec((G, 2, D), lambda i: (i + at, 0, 0)),
            pl.BlockSpec((OUT, D), lambda i: (0, 0)),
        ]
        + [pl.BlockSpec(memory_space=pl.ANY)] * len(more),
        out_specs=[
            pl.BlockSpec((G, TD, D), lambda i: (i + at, 0, 0)),
            pl.BlockSpec((G, 2, D), lambda i: (i, 0, 0)),
        ],
        out_shape=shapes,
        scratch_shapes=[pltpu.VMEM((OUT, D), BF16), pltpu.VMEM((TD, D), F32)],
        input_output_aliases={5: 0} if more else {},
        cost_estimate=pl.CostEstimate(
            flops=40 * FD // PARTS * TD * D, bytes_accessed=5 * FD // PARTS * TD * D, transcendentals=0
        ),
        compiler_params=params(),
        name="hidden_part",
    )(hidden, stats, up, modulation, weight, *more)


def order_kernel(in_ref, out_ref):
    for e in range(NEV):
        out_ref[e * HEAD_ROWS : (e + 1) * HEAD_ROWS, :] = in_ref[place_of(e)]


def order_rows(blocks):
    vmem = pl.BlockSpec(memory_space=pltpu.VMEM)
    return pl.pallas_call(
        order_kernel,
        in_specs=[vmem],
        out_specs=vmem,
        out_shape=jax.ShapeDtypeStruct((OUT, D), F32),
        compiler_params=params(),
        name="order_rows",
    )(blocks)


def far_pairs():
    pairs = []
    for tm in range(NTM):
        for ev in range(NEV):
            y, z = divmod(tm, 8)
            x, c = divmod(ev, 2)
            dest_tm = 8 * x + 4 * c + z % 4
            dest_ev = 2 * ((x + y) % 4) + z // 4
            pairs.append((tm * NEV + ev, dest_tm * NEV + dest_ev))
    return pairs


def eval_flip(value, bit):
    return lax.ppermute(value, "eval", [(i, i ^ bit) for i in range(NEV)])


def swap4(value, axis, groups):
    return lax.all_to_all(value, axis, split_axis=0, concat_axis=0, tiled=True, axis_index_groups=groups)


Z_GROUPS = [[4 * i + j for j in range(4)] for i in range(8)]
X_GROUPS = [[0, 2, 4, 6], [1, 3, 5, 7]]


def per_device(hidden, modulation, head_weight, real_score, fake_score, window_start, timestep):
    both = ("tm", "eval")
    rows = row_table(window_start)
    adapted, stats, pieces = forward(hidden, modulation, head_weight)
    pieces = swap4(pieces, "tm", Z_GROUPS)
    moved = lax.ppermute(pieces.reshape(64, C, BLK), both, far_pairs())
    own = swap4(jnp.broadcast_to(moved[None], (4, 64, C, BLK)), "eval", X_GROUPS).reshape(NF // 2, C, BLK)
    other = eval_flip(own, 1)
    sums = window_sums(rows, own, other, real_score)
    totals = lax.all_to_all(sums, "tm", split_axis=0, concat_axis=0, tiled=True)
    keep, give = window_grads(rows, timestep, totals, real_score, fake_score)
    half = keep + eval_flip(give, 1)
    mine = jnp.sum(swap4(half.reshape(4, 64, C, BLK), "eval", X_GROUPS), axis=0).astype(BF16)
    back = lax.ppermute(mine, both, [(b, a) for a, b in far_pairs()])
    pieces = swap4(back.reshape(4, FD, C, BLK), "tm", Z_GROUPS)
    up, head = head_part(pieces, adapted)
    for bit, size in ((1, 4), (2, 2), (4, 1)):
        head = head[:size] + eval_flip(head[size:], bit)
    d_hidden = None
    parts = []
    for part in range(PARTS):
        d_hidden, red = hidden_part(part, hidden, stats, up, modulation, head_weight, d_hidden)
        parts.append(red)
    mod_grad = jnp.concatenate(parts, axis=0)
    for bit in (1, 2, 4):
        mod_grad = mod_grad + eval_flip(mod_grad, bit)
    for bit in (1, 2, 4, 8, 16):
        head = head + lax.ppermute(head, "tm", [(i, i ^ bit) for i in range(NTM)])
    for bit in (4, 2, 1):
        head = jnp.concatenate([head, eval_flip(head, bit)], axis=0)
    return (d_hidden, order_rows(head), mod_grad)


def solution(mesh):
    placed = (
        P("tm", "eval", None),
        P("tm", None, None),
        P(),
        P("eval", None, None, "tm"),
        P("eval", None, None, "tm"),
        P("eval"),
        P("eval"),
    )
    return jax.shard_map(
        per_device,
        mesh=mesh,
        in_specs=placed,
        out_specs=(P("tm", "eval", None), P(), P("tm", None, None)),
        check_vma=False,
    )
```

```python
import jax
import jax.numpy as jnp
from jax import lax
from jax.experimental import pallas as pl
from jax.experimental.pallas import tpu as pltpu
from jax.sharding import PartitionSpec as P

C = 16
PATCH = 4
OUT = C * PATCH
WIN = 21
TOK = 1024
D = 1536
NTM = 32
NEV = 8
FD = 16
TD = TOK // NEV
PX = TD * PATCH
NF = FD * NTM
BLK = PX // PATCH
FG = 4
HG = 8
G = 2
ROW = 16
BROW = 32
PARTS = 2
NW = 8
HEAD_ROWS = OUT // NEV


F32 = jnp.float32
BF16 = jnp.bfloat16


def params(mib):
    return pltpu.CompilerParams(vmem_limit_bytes=mib * 1024 * 1024)


def dot(a, b, ca=1, cb=0):
    return lax.dot_general(a, b, (((ca,), (cb,)), ((), ())), preferred_element_type=F32)


def build_weight(w_ref, wp_ref):
    row = lax.broadcasted_iota(jnp.int32, (OUT, OUT), 0)
    col = lax.broadcasted_iota(jnp.int32, (OUT, OUT), 1)
    pick = (col == (row % C) * PATCH + row // C).astype(F32).astype(BF16)
    wp_ref[...] = dot(pick, w_ref[...]).astype(BF16)


def build_pixels(e_ref):
    row = lax.broadcasted_iota(jnp.int32, (PX, PX), 0)
    col = lax.broadcasted_iota(jnp.int32, (PX, PX), 1)
    e_ref[...] = (col == (row % TD) * PATCH + row // TD).astype(F32).astype(BF16)


def slot_turn():
    tm = lax.axis_index("tm")
    core = lax.axis_index("eval") % 2
    j, h = tm % 4, (tm // 4) % 2
    return jnp.where(h == core, j, 3 - j)


def forward_kernel(x_ref, mod_ref, w_ref, ad_ref, st_ref, lat_ref, wp_ref, e_ref):
    @pl.when(pl.program_id(0) == 0)
    def _():
        build_weight(w_ref, wp_ref)
        build_pixels(e_ref)

    turn = slot_turn()
    lane = lax.broadcasted_iota(jnp.int32, (ROW, 128), 1)
    for g in range(FG):
        scale = 1.0 + mod_ref[g, 1:2, :]
        shift = mod_ref[g, 0:1, :]
        for q in range(0, TD, ROW):
            x = x_ref[g, q : q + ROW, :].astype(F32)
            m = jnp.mean(x, axis=-1, keepdims=True)
            xc = x - m
            inv = lax.rsqrt(jnp.mean(xc * xc, axis=-1, keepdims=True) + 1e-06)
            st_ref[g, q : q + ROW, :] = jnp.where(lane == 0, m, inv)
            ad_ref[g, q : q + ROW, :] = ((xc * inv) * scale + shift).astype(BF16)
        o = dot(wp_ref[...], ad_ref[g], 1, 1).astype(BF16)
        wide = jnp.concatenate([o[s * C : (s + 1) * C] for s in range(PATCH)], axis=1)
        lat = dot(wide, e_ref[...]).astype(BF16)
        for k in range(4):
            lat_ref[lax.bitwise_xor(turn, k), g] = lat[:, k * BLK : (k + 1) * BLK]


def forward(hidden, modulation, weight):
    return pl.pallas_call(
        forward_kernel,
        grid=(FD // FG,),
        in_specs=[
            pl.BlockSpec((FG, TD, D), lambda i: (i, 0, 0)),
            pl.BlockSpec((FG, 2, D), lambda i: (i, 0, 0)),
            pl.BlockSpec((OUT, D), lambda i: (0, 0)),
        ],
        out_specs=[
            pl.BlockSpec((FG, TD, D), lambda i: (i, 0, 0)),
            pl.BlockSpec((FG, TD, 128), lambda i: (i, 0, 0)),
            pl.BlockSpec((4, FG, C, BLK), lambda i: (0, i, 0, 0)),
        ],
        out_shape=[
            jax.ShapeDtypeStruct((FD, TD, D), BF16),
            jax.ShapeDtypeStruct((FD, TD, 128), F32),
            jax.ShapeDtypeStruct((4, FD, C, BLK), BF16),
        ],
        scratch_shapes=[pltpu.VMEM((OUT, D), BF16), pltpu.VMEM((PX, PX), BF16)],
        compiler_params=params(56),
        name="forward",
    )(hidden, modulation, weight)


def row_tables(starts):
    tm = lax.axis_index("tm")
    ev = lax.axis_index("eval")
    y, zh, zj = tm // 8, (tm // 4) % 2, tm % 4
    x, core = ev // 2, ev % 2
    frame = starts[:, None] + jnp.arange(WIN, dtype=jnp.int32)[None, :]
    owner = frame // FD
    yo, ho, jo = owner // 8, (owner // 4) % 2, owner % 4
    slot = lax.bitwise_xor(lax.bitwise_xor(jo, zj), jnp.where(ho == zh, 0, 3))
    base = (NF // 2) * ((ho + core) % 2) + FD * slot + frame % FD
    block = (2 * y + 6 - yo) % 4
    return base + 64 * block, base + 64 * ((block + 4 - x) % 4)


def sums_kernel(row_ref, own_ref, other_ref, real_ref, out_ref):
    rows = []
    for w in range(NW):
        parts = []
        for t in range(WIN):
            row = row_ref[w, t]
            at = row % (NF // 2)
            latent = jnp.where(row < NF // 2, own_ref[at].astype(F32), other_ref[at].astype(F32))
            parts.append(jnp.abs(latent - real_ref[w, t].astype(F32)))
        while len(parts) > 1:
            parts = [a + b for a, b in zip(parts[::2], parts[1::2])] + ([parts[-1]] if len(parts) % 2 else [])
        rows.append(jnp.sum(parts[0], axis=0, keepdims=True))
    each = jnp.sum(jnp.concatenate(rows, axis=0), axis=1, keepdims=True)
    lane = lax.broadcasted_iota(jnp.int32, (NW, 128), 1)
    place = lax.broadcasted_iota(jnp.int32, (NW, 128), 0)
    total = jnp.sum(jnp.where(lane == place, each, 0.0), axis=0, keepdims=True)
    out_ref[...] = jnp.broadcast_to(total[None], (NTM, 1, 128))


def window_sums(rows, own, other, real):
    return pl.pallas_call(
        sums_kernel,
        in_specs=[
            pl.BlockSpec(memory_space=pltpu.SMEM),
            pl.BlockSpec(memory_space=pltpu.VMEM),
            pl.BlockSpec(memory_space=pltpu.VMEM),
            pl.BlockSpec(memory_space=pltpu.VMEM),
        ],
        out_specs=pl.BlockSpec(memory_space=pltpu.VMEM),
        out_shape=jax.ShapeDtypeStruct((NTM, 1, 128), F32),
        compiler_params=params(40),
        name="window_sums",
    )(rows, own, other, real)


def grads_kernel(row_ref, step_ref, tot_ref, real_ref, fake_ref, own_ref, other_ref, acc_ref, sem):
    lane = lax.broadcasted_iota(jnp.int32, (1, 128), 1)
    totals = jnp.sum(tot_ref[...], axis=0)
    normalizer = totals / (WIN * C * PATCH * TOK) + 1e-05
    level = jnp.zeros((1, 128), F32)
    for w in range(NW):
        level = jnp.where(lane == w, step_ref[w].astype(F32), level)
    weight = level / 1000.0 / normalizer
    acc_ref[...] = jnp.zeros_like(acc_ref)
    for w in range(NW):
        one = jnp.sum(jnp.where(lane == w, weight, 0.0), axis=1, keepdims=True)
        for t in range(WIN):
            acc_ref[row_ref[w, t]] += one * (fake_ref[w, t].astype(F32) - real_ref[w, t].astype(F32))
    copies = [
        pltpu.make_async_copy(acc_ref.at[pl.ds(NF // 2, NF // 2)], other_ref, sem.at[1]),
        pltpu.make_async_copy(acc_ref.at[pl.ds(0, NF // 2)], own_ref, sem.at[0]),
    ]
    for copy in copies:
        copy.start()
    for copy in copies:
        copy.wait()


def window_grads(rows, steps, totals, real, fake):
    smem = pl.BlockSpec(memory_space=pltpu.SMEM)
    vmem = pl.BlockSpec(memory_space=pltpu.VMEM)
    half = jax.ShapeDtypeStruct((NF // 2, C, BLK), F32)
    return pl.pallas_call(
        grads_kernel,
        in_specs=[smem, smem, vmem, vmem, vmem],
        out_specs=[pl.BlockSpec(memory_space=pl.ANY)] * 2,
        out_shape=[half, half],
        scratch_shapes=[pltpu.VMEM((NF, C, BLK), F32), pltpu.SemaphoreType.DMA((2,))],
        compiler_params=params(16),
        name="window_grads",
    )(rows, steps, totals, real, fake)


def holder(place):
    rel = (place >> 2) | (place & 2) | ((place & 1) << 2)
    return lax.bitwise_xor(lax.axis_index("eval"), rel)


def head_kernel(g_ref, ad_ref, up_ref, keep_ref, send_ref, e_ref, acc_ref):
    step = pl.program_id(0)

    @pl.when(step == 0)
    def _():
        build_pixels(e_ref)
        acc_ref[...] = jnp.zeros_like(acc_ref)

    turn = slot_turn()
    ups = []
    for g in range(HG):
        grad = jnp.concatenate([g_ref[lax.bitwise_xor(turn, k), g] for k in range(4)], axis=1)
        wide = dot(grad, e_ref[...], 1, 1).astype(BF16)
        up = jnp.concatenate([wide[:, s * TD : (s + 1) * TD] for s in range(PATCH)], axis=0)
        up_ref[g] = up
        ups.append(up)
    acc_ref[...] += dot(jnp.concatenate(ups, axis=1), ad_ref[...].reshape(HG * TD, D))

    @pl.when(step == pl.num_programs(0) - 1)
    def _():
        for place in range(NEV):
            e = holder(place)
            half = keep_ref if place < NEV // 2 else send_ref
            for i in range(HEAD_ROWS):
                row = (i % PATCH) * C + i // PATCH + (HEAD_ROWS // PATCH) * e
                half[place % (NEV // 2), i : i + 1, :] = acc_ref[pl.ds(row, 1), :]


def head_part(pieces, adapted):
    half = jax.ShapeDtypeStruct((NEV // 2, HEAD_ROWS, D), F32)
    return pl.pallas_call(
        head_kernel,
        grid=(FD // HG,),
        in_specs=[
            pl.BlockSpec((4, HG, C, BLK), lambda i: (0, i, 0, 0)),
            pl.BlockSpec((HG, TD, D), lambda i: (i, 0, 0)),
        ],
        out_specs=[pl.BlockSpec((HG, OUT, TD), lambda i: (i, 0, 0))]
        + [pl.BlockSpec((NEV // 2, HEAD_ROWS, D), lambda i: (0, 0, 0))] * 2,
        out_shape=[jax.ShapeDtypeStruct((FD, OUT, TD), BF16), half, half],
        scratch_shapes=[pltpu.VMEM((PX, PX), BF16), pltpu.VMEM((OUT, D), F32)],
        compiler_params=params(20),
        name="head_part",
    )(pieces, adapted)


def hidden_kernel(x_ref, st_ref, up_ref, mod_ref, w_ref, *refs):
    dh_ref, red_ref, wp_ref, da_ref = refs[-4:]

    @pl.when(pl.program_id(0) == 0)
    def _():
        build_weight(w_ref, wp_ref)

    for g in range(G):
        da_ref[...] = dot(up_ref[g], wp_ref[...], 0, 0)
        scale = 1.0 + mod_ref[g, 1:2, :]
        sum0 = jnp.zeros((BROW, D), F32)
        sum1 = jnp.zeros((BROW, D), F32)
        for q in range(0, TD, BROW):
            d_ad = da_ref[q : q + BROW, :]
            inv = st_ref[g, q : q + BROW, 1:2]
            normed = (x_ref[g, q : q + BROW, :].astype(F32) - st_ref[g, q : q + BROW, 0:1]) * inv
            product = d_ad * normed
            sum0 += d_ad
            sum1 += product
            dn = d_ad * scale
            m1 = jnp.mean(dn, axis=-1, keepdims=True)
            m2 = jnp.mean(product * scale, axis=-1, keepdims=True)
            dh_ref[g, q : q + BROW, :] = (inv * (dn - m1 - normed * m2)).astype(BF16)
        red_ref[g, 0:1, :] = jnp.sum(sum0, axis=0, keepdims=True)
        red_ref[g, 1:2, :] = jnp.sum(sum1, axis=0, keepdims=True)


def hidden_part(part, hidden, stats, up, modulation, weight, so_far, so_far_red):
    count = FD // PARTS // G
    at = part * count
    shapes = [jax.ShapeDtypeStruct((FD, TD, D), BF16), jax.ShapeDtypeStruct((FD, 2, D), F32)]
    more = [] if so_far is None else [so_far, so_far_red]
    return pl.pallas_call(
        hidden_kernel,
        grid=(count,),
        in_specs=[
            pl.BlockSpec((G, TD, D), lambda i: (i + at, 0, 0)),
            pl.BlockSpec((G, TD, 128), lambda i: (i + at, 0, 0)),
            pl.BlockSpec((G, OUT, TD), lambda i: (i + at, 0, 0)),
            pl.BlockSpec((G, 2, D), lambda i: (i + at, 0, 0)),
            pl.BlockSpec((OUT, D), lambda i: (0, 0)),
        ]
        + [pl.BlockSpec(memory_space=pl.ANY)] * len(more),
        out_specs=[
            pl.BlockSpec((G, TD, D), lambda i: (i + at, 0, 0)),
            pl.BlockSpec((G, 2, D), lambda i: (i + at, 0, 0)),
        ],
        out_shape=shapes,
        scratch_shapes=[pltpu.VMEM((OUT, D), BF16), pltpu.VMEM((TD, D), F32)],
        input_output_aliases={5: 0, 6: 1} if more else {},
        cost_estimate=pl.CostEstimate(
            flops=40 * FD // PARTS * TD * D, bytes_accessed=5 * FD // PARTS * TD * D, transcendentals=0
        ),
        compiler_params=params(16),
        name="hidden_part",
    )(hidden, stats, up, modulation, weight, *more)


def order_kernel(*refs):
    out_ref = refs[-1]
    place = 0
    for ref in refs[:-1]:
        for i in range(ref.shape[0]):
            at = pl.multiple_of(HEAD_ROWS * holder(place), HEAD_ROWS)
            out_ref[pl.ds(at, HEAD_ROWS), :] = ref[i]
            place += 1


def order_rows(blocks):
    vmem = pl.BlockSpec(memory_space=pltpu.VMEM)
    return pl.pallas_call(
        order_kernel,
        in_specs=[vmem] * len(blocks),
        out_specs=vmem,
        out_shape=jax.ShapeDtypeStruct((OUT, D), F32),
        compiler_params=params(4),
        name="order_rows",
    )(*blocks)


def far_pairs():
    pairs = []
    for tm in range(NTM):
        for ev in range(NEV):
            y, z = divmod(tm, 8)
            x, c = divmod(ev, 2)
            h, j = divmod(z, 4)
            dest_tm = 8 * x + 4 * c + (j if h == c else 3 - j)
            dest_ev = 2 * ((2 * x - y + 2) % 4) + h
            pairs.append((tm * NEV + ev, dest_tm * NEV + dest_ev))
    return pairs


def x_step(value, steps):
    return lax.ppermute(value, "eval", [(i, (i + 2 * steps) % NEV) for i in range(NEV)])


def near(slots):
    return [slots[0]] + [lax.ppermute(slots[q], "tm", [(i, i ^ q) for i in range(NTM)]) for q in (1, 2, 3)]


def eval_flip(value, bit):
    return lax.ppermute(value, "eval", [(i, i ^ bit) for i in range(NEV)])


def swap4(value, axis, groups):
    return lax.all_to_all(value, axis, split_axis=0, concat_axis=0, tiled=True, axis_index_groups=groups)


X_GROUPS = [[0, 2, 4, 6], [1, 3, 5, 7]]


def per_device(hidden, modulation, head_weight, real_score, fake_score, window_start, timestep):
    both = ("tm", "eval")
    rows, grad_rows = row_tables(window_start)
    adapted, stats, pieces = forward(hidden, modulation, head_weight)
    held = jnp.concatenate(near(lax.ppermute(pieces, both, far_pairs())), axis=0)
    own = swap4(jnp.broadcast_to(held[None], (4, 64, C, BLK)), "eval", X_GROUPS).reshape(NF // 2, C, BLK)
    other = eval_flip(own, 1)
    sums = window_sums(rows, own, other, real_score)
    totals = lax.all_to_all(sums, "tm", split_axis=0, concat_axis=0, tiled=True)
    keep, give = window_grads(grad_rows, timestep, totals, real_score, fake_score)
    got = eval_flip(give, 1)

    def half(i):
        return keep[32 * i : 32 * (i + 1)] + got[32 * i : 32 * (i + 1)]

    four = lax.optimization_barrier((half(4), half(5), half(3), half(6)))
    ahead = x_step(four[0], 1)
    behind = x_step(four[1], -1)
    ahead_direct = x_step(four[2], 1)
    behind_direct = x_step(four[3], -1)
    ahead = x_step(lax.optimization_barrier(half(2) + ahead), 1)
    behind = x_step(lax.optimization_barrier(half(7) + behind), -1)
    mine = [half(0) + behind_direct + ahead, half(1) + ahead_direct + behind]
    mine = jnp.concatenate(mine, axis=0).astype(BF16).reshape(4, FD, C, BLK)
    back = jnp.stack(near(mine), axis=0)
    pieces = lax.ppermute(back, both, [(b, a) for a, b in far_pairs()])
    up, head, send = head_part(pieces, adapted)
    for bit, size in ((1, 4), (2, 2), (4, 1)):
        total = head + eval_flip(send, bit)
        head, send = total[: size // 2], total[size // 2 :]
    head = total
    d_hidden = mod_grad = None
    for part in range(PARTS):
        d_hidden, mod_grad = hidden_part(
            part, hidden, stats, up, modulation, head_weight, d_hidden, mod_grad
        )
    for bit in (1, 2, 4):
        mod_grad = mod_grad + eval_flip(mod_grad, bit)
    for bit in (1, 2, 4, 8, 16):
        moved = lax.ppermute(head, "tm", [(i, i ^ bit) for i in range(NTM)])
        head = head + moved
    blocks = [head]
    for bit in (4, 2, 1):
        blocks.append(eval_flip(jnp.concatenate(blocks, axis=0), bit))
    return (d_hidden, order_rows(blocks), mod_grad)


def solution(mesh):
    placed = (
        P("tm", "eval", None),
        P("tm", None, None),
        P(),
        P("eval", None, None, "tm"),
        P("eval", None, None, "tm"),
        P("eval"),
        P("eval"),
    )
    return jax.shard_map(
        per_device,
        mesh=mesh,
        in_specs=placed,
        out_specs=(P("tm", "eval", None), P(), P("tm", None, None)),
        check_vma=False,
    )
```

```python
import jax
import jax.numpy as jnp
from jax import lax
from jax.experimental import pallas as pl
from jax.experimental.pallas import tpu as pltpu
from jax.sharding import PartitionSpec as P

C = 16
PATCH = 4
OUT = C * PATCH
WIN = 21
TOK = 1024
D = 1536
NTM = 32
NEV = 8
FD = 16
TD = TOK // NEV
PX = TD * PATCH
NF = FD * NTM
BLK = PX // PATCH
FG = 4
HG = 8
G = 2
ROW = 16
BROW = 32
PARTS = 4
NW = 8
HEAD_ROWS = OUT // NEV


F32 = jnp.float32
BF16 = jnp.bfloat16


def params(mib):
    return pltpu.CompilerParams(vmem_limit_bytes=mib * 1024 * 1024)


def dot(a, b, ca=1, cb=0):
    return lax.dot_general(a, b, (((ca,), (cb,)), ((), ())), preferred_element_type=F32)


def build_weight(w_ref, wp_ref):
    row = lax.broadcasted_iota(jnp.int32, (OUT, OUT), 0)
    col = lax.broadcasted_iota(jnp.int32, (OUT, OUT), 1)
    pick = (col == (row % C) * PATCH + row // C).astype(F32).astype(BF16)
    wp_ref[...] = dot(pick, w_ref[...]).astype(BF16)


def build_pixels(e_ref):
    row = lax.broadcasted_iota(jnp.int32, (PX, PX), 0)
    col = lax.broadcasted_iota(jnp.int32, (PX, PX), 1)
    e_ref[...] = (col == (row % TD) * PATCH + row // TD).astype(F32).astype(BF16)


def slot_turn():
    tm = lax.axis_index("tm")
    core = lax.axis_index("eval") % 2
    j, h = tm % 4, (tm // 4) % 2
    return jnp.where(h == core, j, 3 - j)


def forward_kernel(x_ref, mod_ref, w_ref, ad_ref, st_ref, lat_ref, wp_ref, e_ref):
    @pl.when(pl.program_id(0) == 0)
    def _():
        build_weight(w_ref, wp_ref)
        build_pixels(e_ref)

    turn = slot_turn()
    lane = lax.broadcasted_iota(jnp.int32, (ROW, 128), 1)
    for g in range(FG):
        scale = 1.0 + mod_ref[g, 1:2, :]
        shift = mod_ref[g, 0:1, :]
        for q in range(0, TD, ROW):
            x = x_ref[g, q : q + ROW, :].astype(F32)
            m = jnp.mean(x, axis=-1, keepdims=True)
            xc = x - m
            inv = lax.rsqrt(jnp.mean(xc * xc, axis=-1, keepdims=True) + 1e-06)
            st_ref[g, q : q + ROW, :] = jnp.where(lane == 0, m, inv)
            ad_ref[g, q : q + ROW, :] = ((xc * inv) * scale + shift).astype(BF16)
        o = dot(wp_ref[...], ad_ref[g], 1, 1).astype(BF16)
        wide = jnp.concatenate([o[s * C : (s + 1) * C] for s in range(PATCH)], axis=1)
        lat = dot(wide, e_ref[...]).astype(BF16)
        for k in range(4):
            lat_ref[lax.bitwise_xor(turn, k), g] = lat[:, k * BLK : (k + 1) * BLK]


def forward(hidden, modulation, weight):
    return pl.pallas_call(
        forward_kernel,
        grid=(FD // FG,),
        in_specs=[
            pl.BlockSpec((FG, TD, D), lambda i: (i, 0, 0)),
            pl.BlockSpec((FG, 2, D), lambda i: (i, 0, 0)),
            pl.BlockSpec((OUT, D), lambda i: (0, 0)),
        ],
        out_specs=[
            pl.BlockSpec((FG, TD, D), lambda i: (i, 0, 0)),
            pl.BlockSpec((FG, TD, 128), lambda i: (i, 0, 0)),
            pl.BlockSpec((4, FG, C, BLK), lambda i: (0, i, 0, 0)),
        ],
        out_shape=[
            jax.ShapeDtypeStruct((FD, TD, D), BF16),
            jax.ShapeDtypeStruct((FD, TD, 128), F32),
            jax.ShapeDtypeStruct((4, FD, C, BLK), BF16),
        ],
        scratch_shapes=[pltpu.VMEM((OUT, D), BF16), pltpu.VMEM((PX, PX), BF16)],
        compiler_params=params(56),
        name="forward",
    )(hidden, modulation, weight)


def row_tables(starts):
    tm = lax.axis_index("tm")
    ev = lax.axis_index("eval")
    y, zh, zj = tm // 8, (tm // 4) % 2, tm % 4
    x, core = ev // 2, ev % 2
    frame = starts[:, None] + jnp.arange(WIN, dtype=jnp.int32)[None, :]
    owner = frame // FD
    yo, ho, jo = owner // 8, (owner // 4) % 2, owner % 4
    slot = lax.bitwise_xor(lax.bitwise_xor(jo, zj), jnp.where(ho == zh, 0, 3))
    base = (NF // 2) * ((ho + core) % 2) + FD * slot + frame % FD
    block = (2 * y + 6 - yo) % 4
    return base + 64 * block, base + 64 * ((block + 4 - x) % 4)


def sums_kernel(row_ref, own_ref, other_ref, real_ref, out_ref):
    rows = []
    for w in range(NW):
        parts = []
        for t in range(WIN):
            row = row_ref[w, t]
            at = row % (NF // 2)
            latent = jnp.where(row < NF // 2, own_ref[at].astype(F32), other_ref[at].astype(F32))
            parts.append(jnp.abs(latent - real_ref[w, t].astype(F32)))
        while len(parts) > 1:
            parts = [a + b for a, b in zip(parts[::2], parts[1::2])] + ([parts[-1]] if len(parts) % 2 else [])
        rows.append(jnp.sum(parts[0], axis=0, keepdims=True))
    each = jnp.sum(jnp.concatenate(rows, axis=0), axis=1, keepdims=True)
    lane = lax.broadcasted_iota(jnp.int32, (NW, 128), 1)
    place = lax.broadcasted_iota(jnp.int32, (NW, 128), 0)
    total = jnp.sum(jnp.where(lane == place, each, 0.0), axis=0, keepdims=True)
    out_ref[...] = jnp.broadcast_to(total[None], (NTM, 1, 128))


def window_sums(rows, own, other, real):
    return pl.pallas_call(
        sums_kernel,
        in_specs=[
            pl.BlockSpec(memory_space=pltpu.SMEM),
            pl.BlockSpec(memory_space=pltpu.VMEM),
            pl.BlockSpec(memory_space=pltpu.VMEM),
            pl.BlockSpec(memory_space=pltpu.VMEM),
        ],
        out_specs=pl.BlockSpec(memory_space=pltpu.VMEM),
        out_shape=jax.ShapeDtypeStruct((NTM, 1, 128), F32),
        compiler_params=params(40),
        name="window_sums",
    )(rows, own, other, real)


def grads_kernel(row_ref, step_ref, tot_ref, real_ref, fake_ref, own_ref, other_ref, acc_ref, sem):
    lane = lax.broadcasted_iota(jnp.int32, (1, 128), 1)
    totals = jnp.sum(tot_ref[...], axis=0)
    normalizer = totals / (WIN * C * PATCH * TOK) + 1e-05
    level = jnp.zeros((1, 128), F32)
    for w in range(NW):
        level = jnp.where(lane == w, step_ref[w].astype(F32), level)
    weight = level / 1000.0 / normalizer
    acc_ref[...] = jnp.zeros_like(acc_ref)
    for w in range(NW):
        one = jnp.sum(jnp.where(lane == w, weight, 0.0), axis=1, keepdims=True)
        for t in range(WIN):
            acc_ref[row_ref[w, t]] += one * (fake_ref[w, t].astype(F32) - real_ref[w, t].astype(F32))
    copies = [
        pltpu.make_async_copy(acc_ref.at[pl.ds(NF // 2, NF // 2)], other_ref, sem.at[1]),
        pltpu.make_async_copy(acc_ref.at[pl.ds(0, NF // 2)], own_ref, sem.at[0]),
    ]
    for copy in copies:
        copy.start()
    for copy in copies:
        copy.wait()


def window_grads(rows, steps, totals, real, fake):
    smem = pl.BlockSpec(memory_space=pltpu.SMEM)
    vmem = pl.BlockSpec(memory_space=pltpu.VMEM)
    half = jax.ShapeDtypeStruct((NF // 2, C, BLK), F32)
    return pl.pallas_call(
        grads_kernel,
        in_specs=[smem, smem, vmem, vmem, vmem],
        out_specs=[pl.BlockSpec(memory_space=pl.ANY)] * 2,
        out_shape=[half, half],
        scratch_shapes=[pltpu.VMEM((NF, C, BLK), F32), pltpu.SemaphoreType.DMA((2,))],
        compiler_params=params(16),
        name="window_grads",
    )(rows, steps, totals, real, fake)


def holder(place):
    rel = (place >> 2) | (place & 2) | ((place & 1) << 2)
    return lax.bitwise_xor(lax.axis_index("eval"), rel)


def head_kernel(g_ref, ad_ref, up_ref, keep_ref, send_ref, e_ref, acc_ref):
    step = pl.program_id(0)

    @pl.when(step == 0)
    def _():
        build_pixels(e_ref)
        acc_ref[...] = jnp.zeros_like(acc_ref)

    turn = slot_turn()
    ups = []
    for g in range(HG):
        grad = jnp.concatenate([g_ref[lax.bitwise_xor(turn, k), g] for k in range(4)], axis=1)
        wide = dot(grad, e_ref[...], 1, 1).astype(BF16)
        up = jnp.concatenate([wide[:, s * TD : (s + 1) * TD] for s in range(PATCH)], axis=0)
        up_ref[g] = up
        ups.append(up)
    acc_ref[...] += dot(jnp.concatenate(ups, axis=1), ad_ref[...].reshape(HG * TD, D))

    @pl.when(step == pl.num_programs(0) - 1)
    def _():
        for place in range(NEV):
            e = holder(place)
            half = keep_ref if place < NEV // 2 else send_ref
            for i in range(HEAD_ROWS):
                row = (i % PATCH) * C + i // PATCH + (HEAD_ROWS // PATCH) * e
                half[place % (NEV // 2), i : i + 1, :] = acc_ref[pl.ds(row, 1), :]


def head_part(pieces, adapted):
    half = jax.ShapeDtypeStruct((NEV // 2, HEAD_ROWS, D), F32)
    return pl.pallas_call(
        head_kernel,
        grid=(FD // HG,),
        in_specs=[
            pl.BlockSpec((4, HG, C, BLK), lambda i: (0, i, 0, 0)),
            pl.BlockSpec((HG, TD, D), lambda i: (i, 0, 0)),
        ],
        out_specs=[pl.BlockSpec((HG, OUT, TD), lambda i: (i, 0, 0))]
        + [pl.BlockSpec((NEV // 2, HEAD_ROWS, D), lambda i: (0, 0, 0))] * 2,
        out_shape=[jax.ShapeDtypeStruct((FD, OUT, TD), BF16), half, half],
        scratch_shapes=[pltpu.VMEM((PX, PX), BF16), pltpu.VMEM((OUT, D), F32)],
        compiler_params=params(20),
        name="head_part",
    )(pieces, adapted)


def hidden_kernel(x_ref, st_ref, up_ref, mod_ref, w_ref, *refs):
    dh_ref, red_ref, wp_ref, da_ref = refs[-4:]

    @pl.when(pl.program_id(0) == 0)
    def _():
        build_weight(w_ref, wp_ref)

    for g in range(G):
        da_ref[...] = dot(up_ref[g], wp_ref[...], 0, 0)
        scale = 1.0 + mod_ref[g, 1:2, :]
        sum0 = jnp.zeros((BROW, D), F32)
        sum1 = jnp.zeros((BROW, D), F32)
        for q in range(0, TD, BROW):
            d_ad = da_ref[q : q + BROW, :]
            inv = st_ref[g, q : q + BROW, 1:2]
            normed = (x_ref[g, q : q + BROW, :].astype(F32) - st_ref[g, q : q + BROW, 0:1]) * inv
            product = d_ad * normed
            sum0 += d_ad
            sum1 += product
            dn = d_ad * scale
            m1 = jnp.mean(dn, axis=-1, keepdims=True)
            m2 = jnp.mean(product * scale, axis=-1, keepdims=True)
            dh_ref[g, q : q + BROW, :] = (inv * (dn - m1 - normed * m2)).astype(BF16)
        red_ref[g, 0:1, :] = jnp.sum(sum0, axis=0, keepdims=True)
        red_ref[g, 1:2, :] = jnp.sum(sum1, axis=0, keepdims=True)


def hidden_part(part, hidden, stats, up, modulation, weight, so_far, so_far_red):
    count = FD // PARTS // G
    at = part * count
    shapes = [jax.ShapeDtypeStruct((FD, TD, D), BF16), jax.ShapeDtypeStruct((FD, 2, D), F32)]
    more = [] if so_far is None else [so_far, so_far_red]
    return pl.pallas_call(
        hidden_kernel,
        grid=(count,),
        in_specs=[
            pl.BlockSpec((G, TD, D), lambda i: (i + at, 0, 0)),
            pl.BlockSpec((G, TD, 128), lambda i: (i + at, 0, 0)),
            pl.BlockSpec((G, OUT, TD), lambda i: (i + at, 0, 0)),
            pl.BlockSpec((G, 2, D), lambda i: (i + at, 0, 0)),
            pl.BlockSpec((OUT, D), lambda i: (0, 0)),
        ]
        + [pl.BlockSpec(memory_space=pl.ANY)] * len(more),
        out_specs=[
            pl.BlockSpec((G, TD, D), lambda i: (i + at, 0, 0)),
            pl.BlockSpec((G, 2, D), lambda i: (i + at, 0, 0)),
        ],
        out_shape=shapes,
        scratch_shapes=[pltpu.VMEM((OUT, D), BF16), pltpu.VMEM((TD, D), F32)],
        input_output_aliases={5: 0, 6: 1} if more else {},
        cost_estimate=pl.CostEstimate(
            flops=40 * FD // PARTS * TD * D, bytes_accessed=5 * FD // PARTS * TD * D, transcendentals=0
        ),
        compiler_params=params(16),
        name="hidden_part",
    )(hidden, stats, up, modulation, weight, *more)


def order_kernel(*refs):
    out_ref = refs[-1]
    place = 0
    for ref in refs[:-1]:
        for i in range(ref.shape[0]):
            at = pl.multiple_of(HEAD_ROWS * holder(place), HEAD_ROWS)
            out_ref[pl.ds(at, HEAD_ROWS), :] = ref[i]
            place += 1


def order_rows(blocks):
    vmem = pl.BlockSpec(memory_space=pltpu.VMEM)
    return pl.pallas_call(
        order_kernel,
        in_specs=[vmem] * len(blocks),
        out_specs=vmem,
        out_shape=jax.ShapeDtypeStruct((OUT, D), F32),
        compiler_params=params(4),
        name="order_rows",
    )(*blocks)


def far_pairs():
    pairs = []
    for tm in range(NTM):
        for ev in range(NEV):
            y, z = divmod(tm, 8)
            x, c = divmod(ev, 2)
            h, j = divmod(z, 4)
            dest_tm = 8 * x + 4 * c + (j if h == c else 3 - j)
            dest_ev = 2 * ((2 * x - y + 2) % 4) + h
            pairs.append((tm * NEV + ev, dest_tm * NEV + dest_ev))
    return pairs


def x_step(value, steps):
    return lax.ppermute(value, "eval", [(i, (i + 2 * steps) % NEV) for i in range(NEV)])


def near(slots):
    return [slots[0]] + [lax.ppermute(slots[q], "tm", [(i, i ^ q) for i in range(NTM)]) for q in (1, 2, 3)]


def eval_flip(value, bit):
    return lax.ppermute(value, "eval", [(i, i ^ bit) for i in range(NEV)])


def swap4(value, axis, groups):
    return lax.all_to_all(value, axis, split_axis=0, concat_axis=0, tiled=True, axis_index_groups=groups)


X_GROUPS = [[0, 2, 4, 6], [1, 3, 5, 7]]


def per_device(hidden, modulation, head_weight, real_score, fake_score, window_start, timestep):
    both = ("tm", "eval")
    rows, grad_rows = row_tables(window_start)
    adapted, stats, pieces = forward(hidden, modulation, head_weight)
    held = jnp.concatenate(near(lax.ppermute(pieces, both, far_pairs())), axis=0)
    own = swap4(jnp.broadcast_to(held[None], (4, 64, C, BLK)), "eval", X_GROUPS).reshape(NF // 2, C, BLK)
    other = eval_flip(own, 1)
    sums = window_sums(rows, own, other, real_score)
    totals = lax.all_to_all(sums, "tm", split_axis=0, concat_axis=0, tiled=True)
    keep, give = window_grads(grad_rows, timestep, totals, real_score, fake_score)
    got = eval_flip(give, 1)

    def half(i):
        return keep[32 * i : 32 * (i + 1)] + got[32 * i : 32 * (i + 1)]

    four = lax.optimization_barrier((half(4), half(5), half(3), half(6)))
    ahead = x_step(four[0], 1)
    behind = x_step(four[1], -1)
    ahead_direct = x_step(four[2], 1)
    behind_direct = x_step(four[3], -1)
    onward = lax.optimization_barrier((half(2) + ahead, half(7) + behind))
    ahead = x_step(onward[0], 1)
    behind = x_step(onward[1], -1)
    mine = [half(0) + behind_direct + ahead, half(1) + ahead_direct + behind]
    mine = jnp.concatenate(mine, axis=0).astype(BF16).reshape(4, FD, C, BLK)
    back = jnp.stack(near(mine), axis=0)
    pieces = lax.ppermute(back, both, [(b, a) for a, b in far_pairs()])
    up, head, send = head_part(pieces, adapted)
    for bit, size in ((1, 4), (2, 2), (4, 1)):
        total = head + eval_flip(send, bit)
        head, send = total[: size // 2], total[size // 2 :]
    head = total
    d_hidden = mod_grad = None
    for part in range(PARTS):
        d_hidden, mod_grad = hidden_part(
            part, hidden, stats, up, modulation, head_weight, d_hidden, mod_grad
        )
    for bit in (1, 2, 4):
        mod_grad = mod_grad + eval_flip(mod_grad, bit)
    for bit in (1, 2, 4, 8, 16):
        moved = lax.ppermute(head, "tm", [(i, i ^ bit) for i in range(NTM)])
        head = head + moved
    blocks = [head]
    for bit in (4, 2, 1):
        blocks.append(eval_flip(jnp.concatenate(blocks, axis=0), bit))
    return (d_hidden, order_rows(blocks), mod_grad)


def solution(mesh):
    placed = (
        P("tm", "eval", None),
        P("tm", None, None),
        P(),
        P("eval", None, None, "tm"),
        P("eval", None, None, "tm"),
        P("eval"),
        P("eval"),
    )
    return jax.shard_map(
        per_device,
        mesh=mesh,
        in_specs=placed,
        out_specs=(P("tm", "eval", None), P(), P("tm", None, None)),
        check_vma=False,
    )
```
